32 devices in a mesh: group: 16 (over z, y, core), tp: 2 (over x).
Axes of the slice: x: 2, y: 2, z: 4, core: 2. Of those that a mesh axis runs over, the one named last changes fastest.
Arguments:
- tokens: bfloat16 [8192, 3200], P('group', 'tp'), may hold values from -6 to 6
- norm_gain: bfloat16 [3200], P('tp'), may hold values from 0.25 to 1.75
- w_qkv: bfloat16 [3200, 3, 2048], P('group', None, 'tp'), may hold values from -1 to 1, as said below
- qk_gain: float32 [2, 2048], P(None, 'tp'), may hold values from 0.5 to 8
- w_out: bfloat16 [2048, 3200], P('tp', 'group'), may hold values from -0.125 to 0.125
- layer_scale: float32 [3200], P('tp'), may hold values from 0.3 to 1.5
- request: int32 [8192], P('group'), may hold values from 0 to 8191, as said below
- owner: int32 [8192, 1], P('group'), may hold values from 0 to 15; in each aligned block of 512 rows (0 to 511, 512 to 1023, ...) at most 64 rows name the same one
Outputs:
- routed: bfloat16 [16, 16, 64, 3200], P('group', None, None, 'tp')
The draws below stay inside these ranges and needn't reach their ends.
Inputs may be any that keep to these rules, and one draw needn't show every extreme that they name: Requests never cross a block of 1024 rows starting at a multiple of 1024, and blocks share none; in each such block exactly one request holds rows on both sides of its middle, at most 128 on each side, exactly 128 on each side in the first block; the first row's number is 0 and the last row's is 8191. Among one group's 512 rows at most 64 name the same owner; some owner is named by exactly 64 rows of some group. `w_qkv`: column scales of the projections vary across the columns.
All inputs are finite; a program needn't handle non-finite values.
Results may differ from the reference program's by a relative error of at most 0.0117.
The reference program's roundings to bfloat16 on the way count: a program that leaves them out, or rounds other values in their place, can miss the bound.
Values may be sent and summed in bfloat16 or wider, within the bound.
A program may use at most 128 MiB of HBM per device.

```python
import math
import jax
import jax.numpy as jnp
import numpy as np
from jax import lax

D = 3200
HD = 128
HEADS = 16
ROWS = 512
SHARE = 128
CAP = 64
TOKENS = 8192
N_GROUP = 16
N_TP = 2


def draw_w_qkv(key, part):
    width = HEADS * HD
    base = jax.random.truncated_normal(key, -6.0, 6.0, (D, 3, width), jnp.float32)
    column = jnp.arange(width, dtype=jnp.float32) / (width - 1)
    scale = 0.6 + 1.2 * column
    values = base * D ** (-0.5) * scale[None, None, :]
    return jnp.clip(values, -1.0, 1.0).astype(jnp.bfloat16)


def draw_qk_gain(key, part):
    width = HEADS * HD
    unit = jax.random.uniform(key, (2, width), jnp.float32)
    return 0.5 + unit


def draw_request(key, part):
    pairs = N_GROUP // 2
    block = 2 * ROWS
    gap = max(4, ROWS // 3)
    key_cut = jax.random.fold_in(key, 11)
    key_left = jax.random.fold_in(key, 12)
    key_right = jax.random.fold_in(key, 13)
    flags = (jax.random.randint(key_cut, (pairs, block), 0, gap) == 0).astype(jnp.int32)
    position = jnp.arange(block, dtype=jnp.int32)[None, :]
    left = jax.random.randint(key_left, (pairs, 1), 1, SHARE + 1)
    right = jax.random.randint(key_right, (pairs, 1), 1, SHARE + 1)
    left = left.at[0].set(SHARE)
    right = right.at[0].set(SHARE)
    lower = ROWS - left
    upper = ROWS + right
    flags = jnp.where((position > lower) & (position < upper), 0, flags)
    flags = jnp.where((position == lower) | (position == upper), 1, flags)
    flags = flags.at[:, 0].set(0)
    ordinal = jnp.cumsum(flags, axis=1)
    total = ordinal[:, -1:]
    backward = block - 1 - (total - ordinal)
    pair_index = jnp.arange(pairs, dtype=jnp.int32)[:, None]
    local_ids = jnp.where(pair_index == 0, ordinal, backward)
    ids = pair_index * block + local_ids
    return ids.reshape(-1).astype(jnp.int32)


def block_levels(stream_key, dims, split, smallest, top_value):
    factor_of, own = 1.0, jax.random.fold_in(stream_key, 6)
    for dim, parts in split:
        steps = jnp.exp(jax.random.uniform(jax.random.fold_in(own, dim), (parts,), jnp.float32, smallest / len(split), top_value / len(split)))
        factor_of = factor_of * jnp.repeat(steps, dims[dim] // parts).reshape([-1 if axis == dim else 1 for axis in range(len(dims))])
    return factor_of


def routed_block(key, own, number, rows, count, top, most, slope):
    order = jax.random.permutation(key, count)
    crowded, usual = shares(count, rows * top, most, slope, True), shares(count, rows * top, most, slope, False)
    places = jnp.arange(count)

    def named(tallies, offset_by):
        used = int((tallies > 0).sum())
        fixed = max(1, used // 4)
        shifted = fixed + (places - fixed + offset_by * (used - fixed)) % max(1, count - fixed)
        return jnp.zeros((count,), jnp.int32).at[order[jnp.where(places < fixed, places, shifted)]].set(jnp.asarray(tallies, jnp.int32))

    tallies = jnp.where(number % 4 == 0, named(crowded, number // 4), named(usual, number - number // 4 - 1))
    mixed = jax.random.permutation(jax.random.fold_in(own, 3), count)
    source_of, sink = mixed[0:count // 2 * 2:2], mixed[1:count // 2 * 2:2]
    room = jnp.minimum(tallies[source_of] - 1, most - tallies[sink]) // 2
    room = jnp.where((source_of == order[0]) | (sink == order[0]) | (tallies[sink] == 0), 0, jnp.maximum(room, 0))
    shifted = jax.random.randint(jax.random.fold_in(own, 4), (count // 2,), 0, 1 << 20) % (room + 1)
    tallies = tallies.at[source_of].add(-shifted).at[sink].add(shifted)
    labels = jnp.searchsorted(jnp.cumsum(tallies), jnp.arange(rows * top), side="right").astype(jnp.int32)
    grid = labels.reshape(top, rows).T
    grid = grid[jax.random.permutation(jax.random.fold_in(own, 1), rows)]
    offset_by = jax.random.randint(jax.random.fold_in(own, 2), (rows, 1), 0, top)
    return jnp.take_along_axis(grid, (jnp.arange(top)[None, :] + offset_by) % top, axis=1)


def shares(count, total, bound, slope, full):
    weights = [(1 << 20) // math.isqrt(grade ** slope) + 1 for grade in range(1, count + 1)]
    largest = bound if full else min(bound, max(-(-total // count), total * weights[0] // sum(weights)))
    least = 1 if total - largest >= count - 1 else 0
    counts, rest = [largest] + [least] * (count - 1), total - largest - least * (count - 1)
    while rest > 0:
        candidates = [i for i in range(1, count) if counts[i] < largest] or [i for i in range(1, count) if counts[i] < bound]
        mass, remaining = sum([weights[i] for i in candidates]), rest
        for i in candidates:
            extra = min(bound - counts[i], max(1, remaining * weights[i] // mass), rest)
            counts[i] = counts[i] + extra
            rest = rest - extra
    return np.array(counts)


def centred(rng, shape, deviation, most, shards=(), held_as=jnp.bfloat16):
    values = jax.random.normal(rng, shape, jnp.float32) * deviation
    if len(shards) > 0:
        values = block_levels(rng, shape, shards, -0.22, 0.18) * values
    return jnp.clip(values, min=-most, max=most).astype(held_as)


def setup_inputs(seed: int = 0) -> dict:
    keys = jax.random.split(jax.random.key(seed), 9)
    tokens = centred(keys[0], (TOKENS, D), 1.0, 6.0, ((0, 16), (1, 2)))
    norm_gain = jnp.clip(1.0 + 0.15 * jax.random.normal(keys[1], (D,), jnp.float32), 0.25, 1.75).astype(jnp.bfloat16)
    w_qkv = draw_w_qkv(jax.random.fold_in(keys[8], 71), 0)
    qk_gain = draw_qk_gain(jax.random.fold_in(keys[8], 71), 0)
    w_out = centred(keys[4], (HEADS * HD, D), (HEADS * HD) ** -0.5, 0.125, ((0, 2), (1, 16)))
    layer_scale = jnp.clip(jnp.exp(math.log(1.5) - 1.60943787 * jax.random.uniform(keys[5], (D,), jnp.float32) ** block_levels(keys[5], (D,), ((0, 2),), -0.2, 0.2)), 0.3, 1.5)
    request = draw_request(jax.random.fold_in(keys[8], 71), 0)
    owner_keys = jax.random.split(jax.random.fold_in(keys[7], 1), TOKENS // ROWS)
    owner_turns = jax.random.permutation(jax.random.fold_in(keys[7], 3), TOKENS // ROWS)
    owner = jax.vmap(lambda own, number: routed_block(jax.random.fold_in(keys[7], 2), own, number, ROWS, N_GROUP, 1, CAP, 2))(owner_keys, owner_turns).reshape((TOKENS, 1))
    return dict(tokens=tokens, norm_gain=norm_gain, w_qkv=w_qkv, qk_gain=qk_gain, w_out=w_out, layer_scale=layer_scale, request=request, owner=owner)


def pair_rows(start, tokens, norm_gain, w_qkv, qk_gain, w_out, layer_scale, request):
    width = HEADS * HD
    block = 2 * ROWS
    rows_in = lax.dynamic_slice_in_dim(tokens, start, block, 0)
    ids = lax.dynamic_slice_in_dim(request, start, block, 0)
    xf = rows_in.astype(jnp.float32)
    stat = lax.optimization_barrier(jnp.mean(xf * xf, axis=-1, keepdims=True))
    normed = (xf * lax.rsqrt(stat + 1e-06) * norm_gain.astype(jnp.float32)).astype(jnp.bfloat16)
    qkv = jnp.dot(normed, w_qkv.reshape(D, 3 * width), preferred_element_type=jnp.float32).reshape(block, 3, width)
    query = qkv[:, 0, :]
    key_rows = qkv[:, 1, :]
    value = qkv[:, 2, :].astype(jnp.bfloat16)
    qstat = lax.optimization_barrier(jnp.mean(query * query, axis=-1, keepdims=True))
    kstat = lax.optimization_barrier(jnp.mean(key_rows * key_rows, axis=-1, keepdims=True))
    qnorm = (query * lax.rsqrt(qstat + 1e-06) * qk_gain[0]).astype(jnp.bfloat16)
    knorm = (key_rows * lax.rsqrt(kstat + 1e-06) * qk_gain[1]).astype(jnp.bfloat16)
    qh = qnorm.reshape(block, HEADS, HD).astype(jnp.float32)
    kh = knorm.reshape(block, HEADS, HD).astype(jnp.float32)
    vh = value.reshape(block, HEADS, HD).astype(jnp.float32)
    scores = jnp.einsum('qhd,khd->hqk', qh, kh) / math.sqrt(HD)
    same = ids[:, None] == ids[None, :]
    scores = jnp.where(same[None], scores, -jnp.inf)
    top = lax.optimization_barrier(jnp.max(scores, axis=-1, keepdims=True))
    expo = jnp.exp(scores - top)
    probs = (expo / lax.optimization_barrier(jnp.sum(expo, axis=-1, keepdims=True))).astype(jnp.bfloat16)
    attended = jnp.einsum('hqk,khd->qhd', probs.astype(jnp.float32), vh).astype(jnp.bfloat16).reshape(block, width)
    local = width // N_TP
    branch = jnp.zeros((block, D), jnp.float32)
    for piece_index in range(N_TP):
        lo = piece_index * local
        part = jnp.dot(attended[:, lo:lo + local], w_out[lo:lo + local], preferred_element_type=jnp.float32).astype(jnp.bfloat16)
        part = lax.optimization_barrier(part)
        branch = branch + part.astype(jnp.float32)
    return (xf + layer_scale * branch).astype(jnp.bfloat16)

def reference(tokens, norm_gain, w_qkv, qk_gain, w_out, layer_scale, request, owner):
    pairs = N_GROUP // 2
    starts = jnp.arange(pairs, dtype=jnp.int32) * (2 * ROWS)
    mixed = lax.map(lambda s: pair_rows(s, tokens, norm_gain, w_qkv, qk_gain, w_out, layer_scale, request), starts)
    mixed = mixed.reshape(N_GROUP, ROWS, D)
    own = owner[:, 0].reshape(N_GROUP, ROWS)
    onehot = (own[:, :, None] == jnp.arange(N_GROUP, dtype=jnp.int32)[None, None, :]).astype(jnp.int32)
    slot = lax.optimization_barrier(jnp.sum((jnp.cumsum(onehot, axis=1) - onehot) * onehot, axis=-1))
    source = jnp.broadcast_to(jnp.arange(N_GROUP, dtype=jnp.int32)[:, None], (N_GROUP, ROWS))
    routed = jnp.zeros((N_GROUP, N_GROUP, CAP, D), jnp.bfloat16)
    routed = routed.at[source, own, slot].set(mixed)
    return jnp.transpose(routed, (1, 0, 2, 3))
```

```python
import math

import jax
import jax.numpy as jnp
from jax import lax
from jax.sharding import PartitionSpec as P

HD = 128
SHARE = 128


def swapped(value, axis, apart):
    mask = 2**apart
    pairs = [(source, source ^ mask) for source in range(lax.axis_size(axis))]
    return lax.ppermute(value, axis, pairs)


def from_next(value, axis):
    count = lax.axis_size(axis)
    return lax.ppermute(value, axis, [((i + 1) % count, i) for i in range(count)])


def shards(tokens, norm_gain, w_qkv, qk_gain, w_out, layer_scale, request, owner):
    rows, feat_local = tokens.shape
    tp_count = lax.axis_size("tp")
    group_count = lax.axis_size("group")
    local_width = w_qkv.shape[2]
    head_count = local_width // HD
    me_tp = lax.axis_index("tp")
    w_k, w_q = (
        lax.all_gather(w_qkv[:, i, :], "group", axis=0, tiled=True) for i in (1, 0)
    )
    whole = jnp.zeros((rows, feat_local * tp_count), jnp.bfloat16)
    gain_all = jnp.zeros((1, feat_local * tp_count), jnp.bfloat16)
    piece, gain = tokens, norm_gain.reshape(1, feat_local)
    for step in range(tp_count):
        at = ((me_tp + step) % tp_count) * feat_local
        whole = lax.dynamic_update_slice(whole, piece, (0, at))
        gain_all = lax.dynamic_update_slice(gain_all, gain, (0, at))
        if step < tp_count - 1:
            piece, gain = from_next(piece, "tp"), from_next(gain, "tp")
    whole, late_v, late_out = lax.optimization_barrier((whole, w_qkv[:, 2, :], w_out))
    w_v = lax.all_gather(late_v, "group", axis=0, tiled=True)
    per = group_count // tp_count
    pairs = []
    for g in range(group_count):
        for b in range(tp_count):
            t, j = g // per, g % per
            to_g = ((b - t) % tp_count) * per + j
            pairs.append((g * tp_count + b, to_g * tp_count + t))
    w_piece = lax.ppermute(late_out.T, ("group", "tp"), pairs)
    w_o = lax.all_gather(w_piece, "group", axis=0, tiled=True)
    w_o = w_o.reshape(tp_count, feat_local, local_width)
    xwide = whole.astype(jnp.float32)
    stat = jnp.mean(xwide * xwide, axis=-1, keepdims=True)
    normed = (xwide * lax.rsqrt(stat + 1e-06) * gain_all.astype(jnp.float32)).astype(jnp.bfloat16)
    key_rows = jnp.dot(normed, w_k, preferred_element_type=jnp.float32)
    query = jnp.dot(normed, w_q, preferred_element_type=jnp.float32)
    qsum, ksum = lax.psum(
        (jnp.sum(query * query, axis=-1), jnp.sum(key_rows * key_rows, axis=-1)), "tp"
    )
    total_width = local_width * tp_count
    qnorm = (query * lax.rsqrt(qsum / total_width + 1e-06)[:, None] * qk_gain[0]).astype(
        jnp.bfloat16
    )
    knorm = (key_rows * lax.rsqrt(ksum / total_width + 1e-06)[:, None] * qk_gain[1]).astype(
        jnp.bfloat16
    )
    parity = lax.axis_index("group") % 2
    seam = jnp.where(parity == 0, rows - SHARE, 0).astype(jnp.int32)
    key_window = lax.dynamic_slice_in_dim(knorm, seam, SHARE, 0)
    id_window = lax.dynamic_slice_in_dim(request, seam, SHARE, 0)
    paired_key, paired_ids = swapped((key_window, id_window), "group", 0)
    all_keys = jnp.concatenate([knorm, paired_key], axis=0)
    all_ids = jnp.concatenate([request, paired_ids], axis=0)
    qheads = qnorm.reshape(rows, head_count, HD)
    kheads = all_keys.reshape(rows + SHARE, head_count, HD)
    scores = jnp.einsum(
        "qhd,khd->hqk", qheads, kheads, preferred_element_type=jnp.float32
    ) / math.sqrt(HD)
    same = request[:, None] == all_ids[None, :]
    scores = jnp.where(same[None], scores, -jnp.inf)
    top = jnp.max(scores, axis=-1, keepdims=True)
    expo = jnp.exp(scores - top)
    probs = (expo / jnp.sum(expo, axis=-1, keepdims=True)).astype(jnp.bfloat16)

    value = jnp.dot(normed, w_v, preferred_element_type=jnp.float32).astype(jnp.bfloat16)
    value_window = lax.dynamic_slice_in_dim(value, seam, SHARE, 0)
    all_values = jnp.concatenate([value, swapped(value_window, "group", 0)], axis=0)
    vheads = all_values.reshape(rows + SHARE, head_count, HD)
    attended = jnp.einsum("hqk,khd->qhd", probs, vheads, preferred_element_type=jnp.float32)
    attended = attended.astype(jnp.bfloat16).reshape(rows, local_width)

    branch = jnp.zeros((rows, feat_local), jnp.float32)
    for step in range(tp_count):
        onward = from_next(attended, "tp") if step < tp_count - 1 else None
        part = lax.dot_general(
            attended, w_o[step], (((1,), (1,)), ((), ())), preferred_element_type=jnp.float32
        )
        branch = branch + part.astype(jnp.bfloat16).astype(jnp.float32)
        attended = onward
    mixed = (tokens.astype(jnp.float32) + layer_scale * branch).astype(jnp.bfloat16)

    capacity = max(2, 2 * rows // group_count)
    target = owner[:, 0]
    onehot = (target[:, None] == jnp.arange(group_count, dtype=jnp.int32)[None, :]).astype(
        jnp.int32
    )
    slot = jnp.sum((jnp.cumsum(onehot, axis=0) - onehot) * onehot, axis=-1)
    place = target * capacity + slot
    select = (
        jnp.arange(group_count * capacity, dtype=jnp.int32)[:, None] == place[None, :]
    ).astype(jnp.bfloat16)
    outbox = jnp.dot(select, mixed, preferred_element_type=jnp.float32).astype(jnp.bfloat16)
    outbox = outbox.reshape(group_count, capacity, feat_local)
    inbox = lax.all_to_all(outbox, "group", split_axis=0, concat_axis=0, tiled=True)
    return inbox[None]


def solution(mesh):
    in_specs = (
        P("group", "tp"),
        P("tp"),
        P("group", None, "tp"),
        P(None, "tp"),
        P("tp", "group"),
        P("tp"),
        P("group"),
        P("group", None),
    )
    out_specs = P("group", None, None, "tp")
    return jax.shard_map(shards, mesh=mesh, in_specs=in_specs, out_specs=out_specs, check_vma=False)
```

```python
import math

import jax
import jax.numpy as jnp
from jax import lax
from jax.sharding import PartitionSpec as P

HD = 128
SHARE = 128


def swapped(value, axis, apart):
    mask = 2**apart
    pairs = [(source, source ^ mask) for source in range(lax.axis_size(axis))]
    return lax.ppermute(value, axis, pairs)


def from_next(value, axis):
    count = lax.axis_size(axis)
    return lax.ppermute(value, axis, [((i + 1) % count, i) for i in range(count)])


def shards(tokens, norm_gain, w_qkv, qk_gain, w_out, layer_scale, request, owner):
    rows, feat_local = tokens.shape
    tp_count = lax.axis_size("tp")
    group_count = lax.axis_size("group")
    local_width = w_qkv.shape[2]
    head_count = local_width // HD
    me_tp = lax.axis_index("tp")
    w_all = lax.all_gather(
        w_qkv.reshape(w_qkv.shape[0], 3 * local_width), "group", axis=0, tiled=True
    )
    whole = jnp.zeros((rows, feat_local * tp_count), jnp.bfloat16)
    gain_all = jnp.zeros((1, feat_local * tp_count), jnp.bfloat16)
    piece, gain = tokens, norm_gain.reshape(1, feat_local)
    for step in range(tp_count):
        at = ((me_tp + step) % tp_count) * feat_local
        whole = lax.dynamic_update_slice(whole, piece, (0, at))
        gain_all = lax.dynamic_update_slice(gain_all, gain, (0, at))
        if step < tp_count - 1:
            piece, gain = from_next(piece, "tp"), from_next(gain, "tp")
    whole, late_out = lax.optimization_barrier((whole, w_out))
    per = group_count // tp_count
    pairs = []
    for g in range(group_count):
        for b in range(tp_count):
            t, j = g // per, g % per
            to_g = ((b - t) % tp_count) * per + j
            pairs.append((g * tp_count + b, to_g * tp_count + t))
    w_piece = lax.ppermute(late_out.T, ("group", "tp"), pairs)
    w_o = lax.all_gather(w_piece, "group", axis=0, tiled=True)
    w_o = w_o.reshape(tp_count, feat_local, local_width)
    xwide = whole.astype(jnp.float32)
    stat = jnp.mean(xwide * xwide, axis=-1, keepdims=True)
    normed = (xwide * lax.rsqrt(stat + 1e-06) * gain_all.astype(jnp.float32)).astype(jnp.bfloat16)
    qkv = jnp.dot(normed, w_all, preferred_element_type=jnp.float32)
    query = qkv[:, :local_width]
    key_rows = qkv[:, local_width : 2 * local_width]
    value = qkv[:, 2 * local_width :].astype(jnp.bfloat16)
    qsum, ksum = lax.psum(
        (jnp.sum(query * query, axis=-1), jnp.sum(key_rows * key_rows, axis=-1)), "tp"
    )
    total_width = local_width * tp_count
    qnorm = (query * lax.rsqrt(qsum / total_width + 1e-06)[:, None] * qk_gain[0]).astype(
        jnp.bfloat16
    )
    knorm = (key_rows * lax.rsqrt(ksum / total_width + 1e-06)[:, None] * qk_gain[1]).astype(
        jnp.bfloat16
    )
    parity = lax.axis_index("group") % 2
    seam = jnp.where(parity == 0, rows - SHARE, 0).astype(jnp.int32)
    key_window = lax.dynamic_slice_in_dim(knorm, seam, SHARE, 0)
    id_window = lax.dynamic_slice_in_dim(request, seam, SHARE, 0)
    paired_key, paired_ids = swapped((key_window, id_window), "group", 0)
    all_keys = jnp.concatenate([knorm, paired_key], axis=0)
    all_ids = jnp.concatenate([request, paired_ids], axis=0)
    qheads = qnorm.reshape(rows, head_count, HD)
    kheads = all_keys.reshape(rows + SHARE, head_count, HD)
    scores = jnp.einsum(
        "qhd,khd->hqk", qheads, kheads, preferred_element_type=jnp.float32
    ) / math.sqrt(HD)
    same = request[:, None] == all_ids[None, :]
    scores = jnp.where(same[None], scores, -jnp.inf)
    top = jnp.max(scores, axis=-1, keepdims=True)
    expo = jnp.exp(scores - top)
    probs = (expo / jnp.sum(expo, axis=-1, keepdims=True)).astype(jnp.bfloat16)

    value_window = lax.dynamic_slice_in_dim(value, seam, SHARE, 0)
    all_values = jnp.concatenate([value, swapped(value_window, "group", 0)], axis=0)
    vheads = all_values.reshape(rows + SHARE, head_count, HD)
    attended = jnp.einsum("hqk,khd->qhd", probs, vheads, preferred_element_type=jnp.float32)
    attended = attended.astype(jnp.bfloat16).reshape(rows, local_width)

    branch = jnp.zeros((rows, feat_local), jnp.float32)
    for step in range(tp_count):
        onward = from_next(attended, "tp") if step < tp_count - 1 else None
        part = lax.dot_general(
            attended, w_o[step], (((1,), (1,)), ((), ())), preferred_element_type=jnp.float32
        )
        branch = branch + part.astype(jnp.bfloat16).astype(jnp.float32)
        attended = onward
    mixed = (tokens.astype(jnp.float32) + layer_scale * branch).astype(jnp.bfloat16)

    capacity = max(2, 2 * rows // group_count)
    target = owner[:, 0]
    onehot = (target[:, None] == jnp.arange(group_count, dtype=jnp.int32)[None, :]).astype(
        jnp.int32
    )
    slot = jnp.sum((jnp.cumsum(onehot, axis=0) - onehot) * onehot, axis=-1)
    place = target * capacity + slot
    select = (
        jnp.arange(group_count * capacity, dtype=jnp.int32)[:, None] == place[None, :]
    ).astype(jnp.bfloat16)
    outbox = jnp.dot(select, mixed, preferred_element_type=jnp.float32).astype(jnp.bfloat16)
    outbox = outbox.reshape(group_count, capacity, feat_local)
    inbox = lax.all_to_all(outbox, "group", split_axis=0, concat_axis=0, tiled=True)
    return inbox[None]


def solution(mesh):
    in_specs = (
        P("group", "tp"),
        P("tp"),
        P("group", None, "tp"),
        P(None, "tp"),
        P("tp", "group"),
        P("tp"),
        P("group"),
        P("group", None),
    )
    out_specs = P("group", None, None, "tp")
    return jax.shard_map(shards, mesh=mesh, in_specs=in_specs, out_specs=out_specs, check_vma=False)
```

```python
import math

import jax
import jax.numpy as jnp
from jax import lax
from jax.experimental import pallas as pl
from jax.experimental.pallas import tpu as pltpu
from jax.sharding import PartitionSpec as P

HD = 128
SHARE = 128


def swapped(value, axis, apart):
    mask = 2**apart
    pairs = [(source, source ^ mask) for source in range(lax.axis_size(axis))]
    return lax.ppermute(value, axis, pairs)


def from_next(value, axis):
    count = lax.axis_size(axis)
    return lax.ppermute(value, axis, [((i + 1) % count, i) for i in range(count)])


def attend_kernel(q_ref, k_ref, v_ref, kp_ref, vp_ref, row_ref, own_ref, pair_ref, out_ref):
    query = q_ref[...]
    over = (((1,), (1,)), ((), ()))
    scale = 1.0 / math.sqrt(HD)
    near = lax.dot_general(query, k_ref[...], over, preferred_element_type=jnp.float32) * scale
    far = lax.dot_general(query, kp_ref[...], over, preferred_element_type=jnp.float32) * scale
    near = jnp.where(row_ref[...] == own_ref[...], near, -jnp.inf)
    far = jnp.where(row_ref[...] == pair_ref[...], far, -jnp.inf)
    top = jnp.maximum(
        jnp.max(near, axis=-1, keepdims=True), jnp.max(far, axis=-1, keepdims=True)
    )
    near, far = jnp.exp(near - top), jnp.exp(far - top)
    share = 1.0 / (jnp.sum(near, axis=-1, keepdims=True) + jnp.sum(far, axis=-1, keepdims=True))
    near, far = (near * share).astype(jnp.bfloat16), (far * share).astype(jnp.bfloat16)
    total = jnp.dot(near, v_ref[...], preferred_element_type=jnp.float32)
    total += jnp.dot(far, vp_ref[...], preferred_element_type=jnp.float32)
    out_ref[...] = total.astype(jnp.bfloat16)


def attend(query, keys, values, paired_keys, paired_values, ids, paired_ids):
    rows, width = query.shape
    seam = paired_keys.shape[0]
    block = pl.BlockSpec((rows, HD), lambda h: (0, h))
    seam_block = pl.BlockSpec((seam, HD), lambda h: (0, h))
    fixed = lambda shape: pl.BlockSpec(shape, lambda h: (0, 0))
    return pl.pallas_call(
        attend_kernel,
        grid=(width // HD,),
        out_shape=jax.ShapeDtypeStruct((rows, width), jnp.bfloat16),
        in_specs=[
            block, block, block, seam_block, seam_block,
            fixed((rows, 1)), fixed((1, rows)), fixed((1, seam)),
        ],
        out_specs=block,
        compiler_params=pltpu.CompilerParams(vmem_limit_bytes=32 * 2**20),
        cost_estimate=pl.CostEstimate(
            flops=4 * rows * (rows + seam) * width,
            transcendentals=rows * (rows + seam) * width // HD,
            bytes_accessed=8 * rows * width,
        ),
    )(
        query, keys, values, paired_keys, paired_values,
        ids[:, None], ids[None, :], paired_ids[None, :],
    )


def route_kernel(count, place_ref, mixed_ref, out_ref, outbox, send_sem, recv_sem, keep_sem):
    me = lax.axis_index("group")
    capacity = outbox.shape[1]
    rows = mixed_ref.shape[0]
    barrier = pltpu.get_barrier_semaphore()

    @pl.loop(1, count)
    def _(step):
        pl.semaphore_signal(
            barrier, inc=1, device_id={"group": lax.rem(me + step, count)},
            device_id_type=pl.DeviceIdType.MESH,
        )

    pl.semaphore_wait(barrier, count - 1)

    def pick(owner):
        slots = lax.broadcasted_iota(jnp.int32, (capacity, rows), 0) + owner * capacity
        select = (slots == place_ref[...]).astype(jnp.float32).astype(jnp.bfloat16)
        return jnp.dot(select, mixed_ref[...], preferred_element_type=jnp.float32).astype(
            jnp.bfloat16
        )

    def sending(step):
        ahead = 1 + lax.rem(step - 1 + count // 2 - 1, count - 1)
        peer = lax.rem(me + ahead, count)
        return peer, pltpu.make_async_remote_copy(
            src_ref=outbox.at[step],
            dst_ref=out_ref.at[me],
            send_sem=send_sem.at[step],
            recv_sem=recv_sem.at[me],
            device_id={"group": peer},
            device_id_type=pl.DeviceIdType.MESH,
        )

    @pl.loop(1, count)
    def _(step):
        peer, copy = sending(step)
        outbox[step] = pick(peer)
        copy.start()

    outbox[0] = pick(me)
    keep = pltpu.make_async_copy(outbox.at[0], out_ref.at[me], keep_sem)
    keep.start()

    @pl.loop(1, count)
    def _(step):
        source = lax.rem(me + step, count)
        pltpu.make_async_remote_copy(
            src_ref=outbox.at[step],
            dst_ref=out_ref.at[source],
            send_sem=send_sem.at[step],
            recv_sem=recv_sem.at[source],
            device_id={"group": source},
            device_id_type=pl.DeviceIdType.MESH,
        ).wait()

    keep.wait()


def route(place, mixed, count, capacity):
    rows, feat = mixed.shape
    return pl.pallas_call(
        lambda *refs: route_kernel(count, *refs),
        name="route",
        out_shape=jax.ShapeDtypeStruct((count, capacity, feat), jnp.bfloat16),
        in_specs=[pl.BlockSpec(memory_space=pltpu.VMEM)] * 2,
        out_specs=pl.BlockSpec(memory_space=pl.ANY),
        scratch_shapes=[
            pltpu.VMEM((count, capacity, feat), jnp.bfloat16),
            pltpu.SemaphoreType.DMA((count,)),
            pltpu.SemaphoreType.DMA((count,)),
            pltpu.SemaphoreType.DMA,
        ],
        compiler_params=pltpu.CompilerParams(
            collective_id=0, has_side_effects=True, vmem_limit_bytes=32 * 2**20
        ),
        cost_estimate=pl.CostEstimate(
            flops=2 * count * capacity * rows * feat,
            transcendentals=0,
            bytes_accessed=4 * count * capacity * feat,
        ),
    )(place[None, :], mixed)


def shards(tokens, norm_gain, w_qkv, qk_gain, w_out, layer_scale, request, owner):
    rows, feat_local = tokens.shape
    tp_count = lax.axis_size("tp")
    group_count = lax.axis_size("group")
    local_width = w_qkv.shape[2]
    head_count = local_width // HD
    me_tp = lax.axis_index("tp")
    w_all = lax.all_gather(
        w_qkv.reshape(w_qkv.shape[0], 3 * local_width), "group", axis=0, tiled=True
    )
    whole = jnp.zeros((rows, feat_local * tp_count), jnp.bfloat16)
    gain_all = jnp.zeros((1, feat_local * tp_count), jnp.bfloat16)
    piece, gain = tokens, norm_gain.reshape(1, feat_local)
    for step in range(tp_count):
        at = ((me_tp + step) % tp_count) * feat_local
        whole = lax.dynamic_update_slice(whole, piece, (0, at))
        gain_all = lax.dynamic_update_slice(gain_all, gain, (0, at))
        if step < tp_count - 1:
            piece, gain = from_next(piece, "tp"), from_next(gain, "tp")
    whole, late_out = lax.optimization_barrier((whole, w_out))
    per = group_count // tp_count
    pairs = []
    for g in range(group_count):
        for b in range(tp_count):
            t, j = g // per, g % per
            to_g = ((b - t) % tp_count) * per + j
            pairs.append((g * tp_count + b, to_g * tp_count + t))
    w_piece = lax.ppermute(late_out.T, ("group", "tp"), pairs)
    w_o = lax.all_gather(w_piece, "group", axis=0, tiled=True)
    w_o = w_o.reshape(tp_count, feat_local, local_width)
    xwide = whole.astype(jnp.float32)
    stat = jnp.mean(xwide * xwide, axis=-1, keepdims=True)
    normed = (xwide * lax.rsqrt(stat + 1e-06) * gain_all.astype(jnp.float32)).astype(jnp.bfloat16)
    qkv = jnp.dot(normed, w_all, preferred_element_type=jnp.float32)
    query = qkv[:, :local_width]
    key_rows = qkv[:, local_width : 2 * local_width]
    value = qkv[:, 2 * local_width :].astype(jnp.bfloat16)
    qsum, ksum = lax.psum(
        (jnp.sum(query * query, axis=-1), jnp.sum(key_rows * key_rows, axis=-1)), "tp"
    )
    total_width = local_width * tp_count
    qnorm = (query * lax.rsqrt(qsum / total_width + 1e-06)[:, None] * qk_gain[0]).astype(
        jnp.bfloat16
    )
    knorm = (key_rows * lax.rsqrt(ksum / total_width + 1e-06)[:, None] * qk_gain[1]).astype(
        jnp.bfloat16
    )
    parity = lax.axis_index("group") % 2
    seam = jnp.where(parity == 0, rows - SHARE, 0).astype(jnp.int32)
    key_window = lax.dynamic_slice_in_dim(knorm, seam, SHARE, 0)
    id_window = lax.dynamic_slice_in_dim(request, seam, SHARE, 0)
    paired_keys, paired_ids = swapped((key_window, id_window), "group", 0)
    value_window = lax.dynamic_slice_in_dim(value, seam, SHARE, 0)
    paired_values = swapped(value_window, "group", 0)
    attended = attend(qnorm, knorm, value, paired_keys, paired_values, request, paired_ids)

    branch = jnp.zeros((rows, feat_local), jnp.float32)
    for step in range(tp_count):
        onward = from_next(attended, "tp") if step < tp_count - 1 else None
        part = lax.dot_general(
            attended, w_o[step], (((1,), (1,)), ((), ())), preferred_element_type=jnp.float32
        )
        branch = branch + part.astype(jnp.bfloat16).astype(jnp.float32)
        attended = onward
    mixed = (tokens.astype(jnp.float32) + layer_scale * branch).astype(jnp.bfloat16)

    capacity = max(2, 2 * rows // group_count)
    target = owner[:, 0]
    onehot = (target[:, None] == jnp.arange(group_count, dtype=jnp.int32)[None, :]).astype(
        jnp.int32
    )
    slot = jnp.sum((jnp.cumsum(onehot, axis=0) - onehot) * onehot, axis=-1)
    place = target * capacity + slot
    inbox = route(place, mixed, group_count, capacity)
    return inbox[None]


def solution(mesh):
    in_specs = (
        P("group", "tp"),
        P("tp"),
        P("group", None, "tp"),
        P(None, "tp"),
        P("tp", "group"),
        P("tp"),
        P("group"),
        P("group", None),
    )
    out_specs = P("group", None, None, "tp")
    return jax.shard_map(shards, mesh=mesh, in_specs=in_specs, out_specs=out_specs, check_vma=False)
```

```python
import math

import jax
import jax.numpy as jnp
from jax import lax
from jax.experimental import pallas as pl
from jax.experimental.pallas import tpu as pltpu
from jax.sharding import PartitionSpec as P

HD = 128
SHARE = 128


def swapped(value, axis, apart):
    mask = 2**apart
    pairs = [(source, source ^ mask) for source in range(lax.axis_size(axis))]
    return lax.ppermute(value, axis, pairs)


def from_next(value, axis):
    count = lax.axis_size(axis)
    return lax.ppermute(value, axis, [((i + 1) % count, i) for i in range(count)])


def attend_kernel(q_ref, k_ref, v_ref, kp_ref, vp_ref, row_ref, own_ref, pair_ref, out_ref):
    query = q_ref[...]
    over = (((1,), (1,)), ((), ()))
    scale = 1.0 / math.sqrt(HD)
    near = lax.dot_general(query, k_ref[...], over, preferred_element_type=jnp.float32) * scale
    far = lax.dot_general(query, kp_ref[...], over, preferred_element_type=jnp.float32) * scale
    near = jnp.where(row_ref[...] == own_ref[...], near, -jnp.inf)
    far = jnp.where(row_ref[...] == pair_ref[...], far, -jnp.inf)
    top = jnp.maximum(
        jnp.max(near, axis=-1, keepdims=True), jnp.max(far, axis=-1, keepdims=True)
    )
    near, far = jnp.exp(near - top), jnp.exp(far - top)
    share = 1.0 / (jnp.sum(near, axis=-1, keepdims=True) + jnp.sum(far, axis=-1, keepdims=True))
    near, far = (near * share).astype(jnp.bfloat16), (far * share).astype(jnp.bfloat16)
    total = jnp.dot(near, v_ref[...], preferred_element_type=jnp.float32)
    total += jnp.dot(far, vp_ref[...], preferred_element_type=jnp.float32)
    out_ref[...] = total.astype(jnp.bfloat16)


def attend(query, keys, values, paired_keys, paired_values, ids, paired_ids):
    rows, width = query.shape
    seam = paired_keys.shape[0]
    block = pl.BlockSpec((rows, HD), lambda h: (0, h))
    seam_block = pl.BlockSpec((seam, HD), lambda h: (0, h))
    fixed = lambda shape: pl.BlockSpec(shape, lambda h: (0, 0))
    return pl.pallas_call(
        attend_kernel,
        grid=(width // HD,),
        out_shape=jax.ShapeDtypeStruct((rows, width), jnp.bfloat16),
        in_specs=[
            block, block, block, seam_block, seam_block,
            fixed((rows, 1)), fixed((1, rows)), fixed((1, seam)),
        ],
        out_specs=block,
        compiler_params=pltpu.CompilerParams(vmem_limit_bytes=32 * 2**20),
        cost_estimate=pl.CostEstimate(
            flops=4 * rows * (rows + seam) * width,
            transcendentals=rows * (rows + seam) * width // HD,
            bytes_accessed=8 * rows * width,
        ),
    )(
        query, keys, values, paired_keys, paired_values,
        ids[:, None], ids[None, :], paired_ids[None, :],
    )


def route_kernel(count, place_ref, mixed_ref, out_ref, outbox, send_sem, recv_sem, keep_sem):
    me = lax.axis_index("group")
    capacity = outbox.shape[1]
    rows = mixed_ref.shape[0]
    barrier = pltpu.get_barrier_semaphore()

    @pl.loop(1, count)
    def _(step):
        pl.semaphore_signal(
            barrier, inc=1, device_id={"group": lax.rem(me + step, count)},
            device_id_type=pl.DeviceIdType.MESH,
        )

    pl.semaphore_wait(barrier, count - 1)

    def pick(owner):
        slots = lax.broadcasted_iota(jnp.int32, (capacity, rows), 0) + owner * capacity
        select = (slots == place_ref[...]).astype(jnp.float32).astype(jnp.bfloat16)
        return jnp.dot(select, mixed_ref[...], preferred_element_type=jnp.float32).astype(
            jnp.bfloat16
        )

    def sending(step):
        ahead = 1 + lax.rem(step - 1 + count // 2 - 1, count - 1)
        peer = lax.rem(me + ahead, count)
        return peer, pltpu.make_async_remote_copy(
            src_ref=outbox.at[step],
            dst_ref=out_ref.at[me],
            send_sem=send_sem.at[step],
            recv_sem=recv_sem.at[me],
            device_id={"group": peer},
            device_id_type=pl.DeviceIdType.MESH,
        )

    @pl.loop(1, count)
    def _(step):
        peer, copy = sending(step)
        outbox[step] = pick(peer)
        copy.start()

    outbox[0] = pick(me)
    keep = pltpu.make_async_copy(outbox.at[0], out_ref.at[me], keep_sem)
    keep.start()

    @pl.loop(1, count)
    def _(step):
        source = lax.rem(me + step, count)
        pltpu.make_async_remote_copy(
            src_ref=outbox.at[step],
            dst_ref=out_ref.at[source],
            send_sem=send_sem.at[step],
            recv_sem=recv_sem.at[source],
            device_id={"group": source},
            device_id_type=pl.DeviceIdType.MESH,
        ).wait()

    keep.wait()


def route(place, mixed, count, capacity):
    rows, feat = mixed.shape
    return pl.pallas_call(
        lambda *refs: route_kernel(count, *refs),
        name="route",
        out_shape=jax.ShapeDtypeStruct((count, capacity, feat), jnp.bfloat16),
        in_specs=[pl.BlockSpec(memory_space=pltpu.VMEM)] * 2,
        out_specs=pl.BlockSpec(memory_space=pl.ANY),
        scratch_shapes=[
            pltpu.VMEM((count, capacity, feat), jnp.bfloat16),
            pltpu.SemaphoreType.DMA((count,)),
            pltpu.SemaphoreType.DMA((count,)),
            pltpu.SemaphoreType.DMA,
        ],
        compiler_params=pltpu.CompilerParams(
            collective_id=0, has_side_effects=True, vmem_limit_bytes=32 * 2**20
        ),
        cost_estimate=pl.CostEstimate(
            flops=2 * count * capacity * rows * feat,
            transcendentals=0,
            bytes_accessed=4 * count * capacity * feat,
        ),
    )(place[None, :], mixed)


def shards(tokens, norm_gain, w_qkv, qk_gain, w_out, layer_scale, request, owner):
    rows, feat_local = tokens.shape
    tp_count = lax.axis_size("tp")
    group_count = lax.axis_size("group")
    local_width = w_qkv.shape[2]
    head_count = local_width // HD
    me_tp = lax.axis_index("tp")
    w_all = lax.all_gather(
        w_qkv.reshape(w_qkv.shape[0], 3 * local_width), "group", axis=0, tiled=True
    )
    whole = jnp.zeros((rows, feat_local * tp_count), jnp.bfloat16)
    gain_all = jnp.zeros((1, feat_local * tp_count), jnp.bfloat16)
    piece, gain = tokens, norm_gain.reshape(1, feat_local)
    for step in range(tp_count):
        at = ((me_tp + step) % tp_count) * feat_local
        whole = lax.dynamic_update_slice(whole, piece, (0, at))
        gain_all = lax.dynamic_update_slice(gain_all, gain, (0, at))
        if step < tp_count - 1:
            piece, gain = from_next(piece, "tp"), from_next(gain, "tp")
    whole, late_out = lax.optimization_barrier((whole, w_out))
    per = group_count // tp_count
    pairs = []
    for g in range(group_count):
        for b in range(tp_count):
            t, j = g // per, g % per
            to_g = b * per + j
            pairs.append((g * tp_count + b, to_g * tp_count + t))
    w_piece = lax.ppermute(late_out.T, ("group", "tp"), pairs)
    w_o = lax.all_gather(w_piece, "group", axis=0, tiled=True)
    w_o = w_o.reshape(tp_count, feat_local, local_width)
    xwide = whole.astype(jnp.float32)
    stat = jnp.mean(xwide * xwide, axis=-1, keepdims=True)
    normed = (xwide * lax.rsqrt(stat + 1e-06) * gain_all.astype(jnp.float32)).astype(jnp.bfloat16)
    qkv = jnp.dot(normed, w_all, preferred_element_type=jnp.float32)
    query = qkv[:, :local_width]
    key_rows = qkv[:, local_width : 2 * local_width]
    value = qkv[:, 2 * local_width :].astype(jnp.bfloat16)
    qsum, ksum = lax.psum(
        (jnp.sum(query * query, axis=-1), jnp.sum(key_rows * key_rows, axis=-1)), "tp"
    )
    total_width = local_width * tp_count
    qnorm = (query * lax.rsqrt(qsum / total_width + 1e-06)[:, None] * qk_gain[0]).astype(
        jnp.bfloat16
    )
    knorm = (key_rows * lax.rsqrt(ksum / total_width + 1e-06)[:, None] * qk_gain[1]).astype(
        jnp.bfloat16
    )
    parity = lax.axis_index("group") % 2
    seam = jnp.where(parity == 0, rows - SHARE, 0).astype(jnp.int32)
    key_window = lax.dynamic_slice_in_dim(knorm, seam, SHARE, 0)
    id_window = lax.dynamic_slice_in_dim(request, seam, SHARE, 0)
    paired_keys, paired_ids = swapped((key_window, id_window), "group", 0)
    value_window = lax.dynamic_slice_in_dim(value, seam, SHARE, 0)
    paired_values = swapped(value_window, "group", 0)
    attended = attend(qnorm, knorm, value, paired_keys, paired_values, request, paired_ids)

    branch = jnp.zeros((rows, feat_local), jnp.float32)
    for step in range(tp_count):
        onward = from_next(attended, "tp") if step < tp_count - 1 else None
        part = lax.dot_general(
            attended,
            lax.dynamic_index_in_dim(w_o, (me_tp + step) % tp_count, 0, keepdims=False),
            (((1,), (1,)), ((), ())),
            preferred_element_type=jnp.float32,
        )
        branch = branch + part.astype(jnp.bfloat16).astype(jnp.float32)
        attended = onward
    mixed = (tokens.astype(jnp.float32) + layer_scale * branch).astype(jnp.bfloat16)

    capacity = max(2, 2 * rows // group_count)
    target = owner[:, 0]
    onehot = (target[:, None] == jnp.arange(group_count, dtype=jnp.int32)[None, :]).astype(
        jnp.int32
    )
    slot = jnp.sum((jnp.cumsum(onehot, axis=0) - onehot) * onehot, axis=-1)
    place = target * capacity + slot
    inbox = route(place, mixed, group_count, capacity)
    return inbox[None]


def solution(mesh):
    in_specs = (
        P("group", "tp"),
        P("tp"),
        P("group", None, "tp"),
        P(None, "tp"),
        P("tp", "group"),
        P("tp"),
        P("group"),
        P("group", None),
    )
    out_specs = P("group", None, None, "tp")
    return jax.shard_map(shards, mesh=mesh, in_specs=in_specs, out_specs=out_specs, check_vma=False)
```

```python
import math

import jax
import jax.numpy as jnp
from jax import lax
from jax.experimental import pallas as pl
from jax.experimental.pallas import tpu as pltpu
from jax.sharding import PartitionSpec as P

HD = 128
SHARE = 128


def swapped(value, axis, apart):
    mask = 2**apart
    pairs = [(source, source ^ mask) for source in range(lax.axis_size(axis))]
    return lax.ppermute(value, axis, pairs)


def from_next(value, axis):
    count = lax.axis_size(axis)
    return lax.ppermute(value, axis, [((i + 1) % count, i) for i in range(count)])


def attend_kernel(q_ref, k_ref, v_ref, kp_ref, vp_ref, row_ref, own_ref, pair_ref, out_ref):
    query = q_ref[...]
    over = (((1,), (1,)), ((), ()))
    scale = 1.0 / math.sqrt(HD)
    near = lax.dot_general(query, k_ref[...], over, preferred_element_type=jnp.float32) * scale
    far = lax.dot_general(query, kp_ref[...], over, preferred_element_type=jnp.float32) * scale
    near = jnp.where(row_ref[...] == own_ref[...], near, -jnp.inf)
    far = jnp.where(row_ref[...] == pair_ref[...], far, -jnp.inf)
    top = jnp.maximum(
        jnp.max(near, axis=-1, keepdims=True), jnp.max(far, axis=-1, keepdims=True)
    )
    near, far = jnp.exp(near - top), jnp.exp(far - top)
    share = 1.0 / (jnp.sum(near, axis=-1, keepdims=True) + jnp.sum(far, axis=-1, keepdims=True))
    near, far = (near * share).astype(jnp.bfloat16), (far * share).astype(jnp.bfloat16)
    total = jnp.dot(near, v_ref[...], preferred_element_type=jnp.float32)
    total += jnp.dot(far, vp_ref[...], preferred_element_type=jnp.float32)
    out_ref[...] = total.astype(jnp.bfloat16)


def attend(query, keys, values, paired_keys, paired_values, ids, paired_ids):
    rows, width = query.shape
    seam = paired_keys.shape[0]
    block = pl.BlockSpec((rows, HD), lambda h: (0, h))
    seam_block = pl.BlockSpec((seam, HD), lambda h: (0, h))
    fixed = lambda shape: pl.BlockSpec(shape, lambda h: (0, 0))
    return pl.pallas_call(
        attend_kernel,
        grid=(width // HD,),
        out_shape=jax.ShapeDtypeStruct((rows, width), jnp.bfloat16),
        in_specs=[
            block, block, block, seam_block, seam_block,
            fixed((rows, 1)), fixed((1, rows)), fixed((1, seam)),
        ],
        out_specs=block,
        compiler_params=pltpu.CompilerParams(vmem_limit_bytes=32 * 2**20),
        cost_estimate=pl.CostEstimate(
            flops=4 * rows * (rows + seam) * width,
            transcendentals=rows * (rows + seam) * width // HD,
            bytes_accessed=8 * rows * width,
        ),
    )(
        query, keys, values, paired_keys, paired_values,
        ids[:, None], ids[None, :], paired_ids[None, :],
    )


def flipped(index, mask, count):
    if count & (count - 1):
        return lax.rem(index + mask, count)
    bits = range(count.bit_length() - 1)
    return sum(
        lax.rem(lax.div(index, 2**bit) + lax.div(mask, 2**bit), 2) * 2**bit for bit in bits
    )


def route_kernel(count, place_ref, mixed_ref, out_ref, outbox, send_sem, recv_sem, keep_sem):
    me = lax.axis_index("group")
    capacity = outbox.shape[1]
    rows = mixed_ref.shape[0]
    barrier = pltpu.get_barrier_semaphore()

    @pl.loop(1, count)
    def _(step):
        pl.semaphore_signal(
            barrier, inc=1, device_id={"group": lax.rem(me + step, count)},
            device_id_type=pl.DeviceIdType.MESH,
        )

    pl.semaphore_wait(barrier, count - 1)

    def pick(owner):
        slots = lax.broadcasted_iota(jnp.int32, (capacity, rows), 0) + owner * capacity
        select = (slots == place_ref[...]).astype(jnp.float32).astype(jnp.bfloat16)
        return jnp.dot(select, mixed_ref[...], preferred_element_type=jnp.float32).astype(
            jnp.bfloat16
        )

    def sending(step):
        peer = flipped(me, count - step, count)
        return peer, pltpu.make_async_remote_copy(
            src_ref=outbox.at[step],
            dst_ref=out_ref.at[me],
            send_sem=send_sem.at[step],
            recv_sem=recv_sem.at[me],
            device_id={"group": peer},
            device_id_type=pl.DeviceIdType.MESH,
        )

    @pl.loop(1, count)
    def _(step):
        peer, copy = sending(step)
        outbox[step] = pick(peer)
        copy.start()

    outbox[0] = pick(me)
    keep = pltpu.make_async_copy(outbox.at[0], out_ref.at[me], keep_sem)
    keep.start()

    @pl.loop(1, count)
    def _(step):
        source = lax.rem(me + step, count)
        pltpu.make_async_remote_copy(
            src_ref=outbox.at[step],
            dst_ref=out_ref.at[source],
            send_sem=send_sem.at[step],
            recv_sem=recv_sem.at[source],
            device_id={"group": source},
            device_id_type=pl.DeviceIdType.MESH,
        ).wait()

    keep.wait()


def route(place, mixed, count, capacity):
    rows, feat = mixed.shape
    return pl.pallas_call(
        lambda *refs: route_kernel(count, *refs),
        name="route",
        out_shape=jax.ShapeDtypeStruct((count, capacity, feat), jnp.bfloat16),
        in_specs=[pl.BlockSpec(memory_space=pltpu.VMEM)] * 2,
        out_specs=pl.BlockSpec(memory_space=pl.ANY),
        scratch_shapes=[
            pltpu.VMEM((count, capacity, feat), jnp.bfloat16),
            pltpu.SemaphoreType.DMA((count,)),
            pltpu.SemaphoreType.DMA((count,)),
            pltpu.SemaphoreType.DMA,
        ],
        compiler_params=pltpu.CompilerParams(
            collective_id=0, has_side_effects=True, vmem_limit_bytes=32 * 2**20
        ),
        cost_estimate=pl.CostEstimate(
            flops=2 * count * capacity * rows * feat,
            transcendentals=0,
            bytes_accessed=4 * count * capacity * feat,
        ),
    )(place[None, :], mixed)


def shards(tokens, norm_gain, w_qkv, qk_gain, w_out, layer_scale, request, owner):
    rows, feat_local = tokens.shape
    tp_count = lax.axis_size("tp")
    group_count = lax.axis_size("group")
    local_width = w_qkv.shape[2]
    head_count = local_width // HD
    me_tp = lax.axis_index("tp")
    w_all = lax.all_gather(
        w_qkv.reshape(w_qkv.shape[0], 3 * local_width), "group", axis=0, tiled=True
    )
    whole = jnp.zeros((rows, feat_local * tp_count), jnp.bfloat16)
    gain_all = jnp.zeros((1, feat_local * tp_count), jnp.bfloat16)
    piece, gain = tokens, norm_gain.reshape(1, feat_local)
    for step in range(tp_count):
        at = ((me_tp + step) % tp_count) * feat_local
        whole = lax.dynamic_update_slice(whole, piece, (0, at))
        gain_all = lax.dynamic_update_slice(gain_all, gain, (0, at))
        if step < tp_count - 1:
            piece, gain = from_next(piece, "tp"), from_next(gain, "tp")
    whole, late_out = lax.optimization_barrier((whole, w_out))
    per = group_count // tp_count
    pairs = []
    for g in range(group_count):
        for b in range(tp_count):
            t, j = g // per, g % per
            to_g = b * per + j
            pairs.append((g * tp_count + b, to_g * tp_count + t))
    w_piece = lax.ppermute(late_out.T, ("group", "tp"), pairs)
    w_o = lax.all_gather(w_piece, "group", axis=0, tiled=True)
    w_o = w_o.reshape(tp_count, feat_local, local_width)
    xwide = whole.astype(jnp.float32)
    stat = jnp.mean(xwide * xwide, axis=-1, keepdims=True)
    normed = (xwide * lax.rsqrt(stat + 1e-06) * gain_all.astype(jnp.float32)).astype(jnp.bfloat16)
    qkv = jnp.dot(normed, w_all, preferred_element_type=jnp.float32)
    query = qkv[:, :local_width]
    key_rows = qkv[:, local_width : 2 * local_width]
    value = qkv[:, 2 * local_width :].astype(jnp.bfloat16)
    qsum, ksum = lax.psum(
        (jnp.sum(query * query, axis=-1), jnp.sum(key_rows * key_rows, axis=-1)), "tp"
    )
    total_width = local_width * tp_count
    qnorm = (query * lax.rsqrt(qsum / total_width + 1e-06)[:, None] * qk_gain[0]).astype(
        jnp.bfloat16
    )
    knorm = (key_rows * lax.rsqrt(ksum / total_width + 1e-06)[:, None] * qk_gain[1]).astype(
        jnp.bfloat16
    )
    parity = lax.axis_index("group") % 2
    seam = jnp.where(parity == 0, rows - SHARE, 0).astype(jnp.int32)
    key_window = lax.dynamic_slice_in_dim(knorm, seam, SHARE, 0)
    id_window = lax.dynamic_slice_in_dim(request, seam, SHARE, 0)
    paired_keys, paired_ids = swapped((key_window, id_window), "group", 0)
    value_window = lax.dynamic_slice_in_dim(value, seam, SHARE, 0)
    paired_values = swapped(value_window, "group", 0)
    attended = attend(qnorm, knorm, value, paired_keys, paired_values, request, paired_ids)

    branch = jnp.zeros((rows, feat_local), jnp.float32)
    for step in range(tp_count):
        onward = from_next(attended, "tp") if step < tp_count - 1 else None
        part = lax.dot_general(
            attended,
            lax.dynamic_index_in_dim(w_o, (me_tp + step) % tp_count, 0, keepdims=False),
            (((1,), (1,)), ((), ())),
            preferred_element_type=jnp.float32,
        )
        branch = branch + part.astype(jnp.bfloat16).astype(jnp.float32)
        attended = onward
    mixed = (tokens.astype(jnp.float32) + layer_scale * branch).astype(jnp.bfloat16)

    capacity = max(2, 2 * rows // group_count)
    target = owner[:, 0]
    onehot = (target[:, None] == jnp.arange(group_count, dtype=jnp.int32)[None, :]).astype(
        jnp.int32
    )
    slot = jnp.sum((jnp.cumsum(onehot, axis=0) - onehot) * onehot, axis=-1)
    place = target * capacity + slot
    inbox = route(place, mixed, group_count, capacity)
    return inbox[None]


def solution(mesh):
    in_specs = (
        P("group", "tp"),
        P("tp"),
        P("group", None, "tp"),
        P(None, "tp"),
        P("tp", "group"),
        P("tp"),
        P("group"),
        P("group", None),
    )
    out_specs = P("group", None, None, "tp")
    return jax.shard_map(shards, mesh=mesh, in_specs=in_specs, out_specs=out_specs, check_vma=False)
```
